128 devices in a mesh: grp: 4 (over y), seq: 32 (over z, x, core).
Axes of the slice: x: 4, y: 4, z: 4, core: 2. Of those that a mesh axis runs over, the one named last changes fastest.
Arguments:
- tiles: bfloat16 [8, 16384, 768], P('grp', 'seq'), may hold values from -8 to 8
- counts: int32 [8], P('grp'), may hold values from 4096 to 16384, as said below
- ln1_gain: float32 [768], replicated, may hold values from 0.1 to 1.9
- qkv_weight: bfloat16 [768, 2304], replicated, may hold values from -0.18042196 to 0.18042196
- out_weight: bfloat16 [768, 768], replicated, may hold values from -0.21875 to 0.21875
- ln2_gain: float32 [768], replicated, may hold values from 0.1 to 1.9
- ff_in: bfloat16 [768, 3072], replicated, may hold values from -0.21875 to 0.21875
- ff_out: bfloat16 [3072, 768], replicated, may hold values from -0.109375 to 0.109375
- pool_weight: bfloat16 [768, 768], P('grp'), may hold values from -0.18042196 to 0.18042196
- class_weight: float32 [384, 8], replicated, may hold values from -3 to 6
Outputs:
- encoded: bfloat16 [8, 16384, 768], P('grp', 'seq')
- pooled: float32 [8, 8, 768], P('grp')
The draws below stay inside these ranges and needn't reach their ends.
Inputs may be any that keep to these rules, and one draw needn't show every extreme that they name: The valid tiles of a slide are its first counts tiles in scan order; some slide has all 16384 tiles valid.
All inputs are finite; a program needn't handle non-finite values.
Results may differ from the reference program's by a relative error of at most 0.015.
Values may be sent and summed in bfloat16 or wider, within the bound.
No kernel may reach another device: no remote copies, remote signals or barrier semaphores. Data moves between devices by JAX's collectives and lax.ppermute only.
A program may use at most 128 MiB of HBM per device.

```python
import jax
import jax.numpy as jnp
from jax import lax

D = 768
HEADS = 16
FF = 3072
ATT_H = 384
CLASSES = 8
BLOCK = 256
SLIDES = 8
TILES = 16384
N_SEQ = 32


def draw_counts(key, part):
    values = jax.random.randint(jax.random.fold_in(key, 11), (SLIDES,), TILES // 4, TILES + 1)
    chosen = jax.random.randint(jax.random.fold_in(key, 17), (), 0, SLIDES)
    return jnp.where(jnp.arange(SLIDES) == chosen, TILES, values).astype(jnp.int32)


def draw_tiles(key, part):
    shape = (SLIDES, TILES, D)
    values = jax.random.truncated_normal(jax.random.fold_in(key, 21), -6.0, 6.0, shape, jnp.float32)
    return values.astype(jnp.bfloat16)


def draw_qkv_weight(key, part):
    shape = (D, 3 * D)
    values = jax.random.truncated_normal(jax.random.fold_in(key, 31), -4.0, 4.0, shape, jnp.float32) * D ** (-0.5)
    return values.astype(jnp.bfloat16)


def draw_pool_weight(key, part):
    shape = (D, 2 * ATT_H)
    values = jax.random.truncated_normal(jax.random.fold_in(key, 41), -4.0, 4.0, shape, jnp.float32) * D ** (-0.5)
    return values.astype(jnp.bfloat16)


def draw_class_weight(key, part):
    shape = (ATT_H, CLASSES)
    values = jax.random.truncated_normal(jax.random.fold_in(key, 51), -6.0, 6.0, shape, jnp.float32) * 0.5
    return values.astype(jnp.float32)


def noise(rng, dims, deviation, most, kind=jnp.bfloat16):
    entries = jax.random.normal(rng, dims, jnp.float32) * deviation
    return jnp.minimum(jnp.maximum(entries, -most), most).astype(kind)


def setup_inputs(seed: int = 0) -> dict:
    splits = jax.random.split(jax.random.key(seed), 11)
    return {
        "tiles": draw_tiles(jax.random.fold_in(splits[10], 71), 0),
        "counts": draw_counts(jax.random.fold_in(splits[10], 71), 0),
        "ln1_gain": jnp.clip(1.0 + 0.18 * jax.random.normal(splits[2], (D,), jnp.float32), 0.1, 1.9),
        "qkv_weight": draw_qkv_weight(jax.random.fold_in(splits[10], 71), 0),
        "out_weight": noise(splits[4], (D, D), D ** -0.5, 0.21875),
        "ln2_gain": jnp.clip(1.0 + 0.18 * jax.random.normal(splits[5], (D,), jnp.float32), 0.1, 1.9),
        "ff_in": noise(splits[6], (D, FF), D ** -0.5, 0.21875),
        "ff_out": noise(splits[7], (FF, D), FF ** -0.5, 0.109375),
        "pool_weight": draw_pool_weight(jax.random.fold_in(splits[10], 71), 0),
        "class_weight": draw_class_weight(jax.random.fold_in(splits[10], 71), 0),
    }


def normalize(values, gain):
    xf = values.astype(jnp.float32)
    centre = lax.optimization_barrier(jnp.mean(xf, axis=-1, keepdims=True))
    spread = lax.optimization_barrier(jnp.mean((xf - centre) ** 2, axis=-1, keepdims=True))
    return (xf - centre) * lax.rsqrt(spread + 1e-05) * gain

def attend(query, key_rows, value_rows, keep):
    scale = 1.0 / query.shape[-1] ** 0.5
    scores = jnp.einsum('qhd,khd->hqk', query.astype(jnp.float32), key_rows.astype(jnp.float32)) * scale
    scores = jnp.where(keep[None, None, :], scores, -1e+30)
    peak = lax.optimization_barrier(jnp.max(scores, axis=-1))
    probs = jnp.exp(scores - peak[..., None])
    total = lax.optimization_barrier(jnp.sum(probs, axis=-1))
    weights = probs.astype(jnp.bfloat16).astype(jnp.float32)
    result = jnp.einsum('hqk,khd->qhd', weights, value_rows.astype(jnp.float32)) / total.T[..., None]
    return (result, (peak + jnp.log(total)).T)

def one_slide(args):
    tiles, count, ln1_gain, qkv_weight, out_weight, ln2_gain, ff_in, ff_out, pool_weight, class_weight = args
    rows = tiles.shape[0]
    width = tiles.shape[1]
    head_dim = width // HEADS
    valid = jnp.arange(rows, dtype=jnp.int32) < count
    normed = normalize(tiles, ln1_gain).astype(jnp.bfloat16)
    proj = jnp.dot(normed, qkv_weight, preferred_element_type=jnp.float32).astype(jnp.bfloat16)
    query = proj[:, :width].reshape(rows, HEADS, head_dim)
    key_rows = proj[:, width:2 * width].reshape(rows, HEADS, head_dim)
    value_rows = proj[:, 2 * width:].reshape(rows, HEADS, head_dim)
    nblocks = rows // BLOCK

    def near(item):
        return attend(item[0], item[1], item[2], item[3])
    near_out, near_lse = lax.map(near, (query.reshape(nblocks, BLOCK, HEADS, head_dim), key_rows.reshape(nblocks, BLOCK, HEADS, head_dim), value_rows.reshape(nblocks, BLOCK, HEADS, head_dim), valid.reshape(nblocks, BLOCK)))
    near_out = near_out.reshape(rows, HEADS, head_dim)
    near_lse = near_lse.reshape(rows, HEADS)
    rate = N_SEQ
    per_class = rows // rate

    def regroup(arr):
        return jnp.swapaxes(arr.reshape((per_class, rate) + arr.shape[1:]), 0, 1)
    far_out, far_lse = lax.map(near, (regroup(query), regroup(key_rows), regroup(value_rows), regroup(valid)))
    far_out = jnp.swapaxes(far_out, 0, 1).reshape(rows, HEADS, head_dim)
    far_lse = jnp.swapaxes(far_lse, 0, 1).reshape(rows, HEADS)
    far_out = lax.optimization_barrier(far_out.astype(jnp.bfloat16)).astype(jnp.float32)
    top = jnp.maximum(near_lse, far_lse)
    near_w = jnp.exp(near_lse - top)
    far_w = jnp.exp(far_lse - top)
    mixed = (near_w[..., None] * near_out + far_w[..., None] * far_out) / (near_w + far_w)[..., None]
    mixed = mixed.reshape(rows, width).astype(jnp.bfloat16)
    resid = tiles.astype(jnp.float32) + jnp.dot(mixed, out_weight, preferred_element_type=jnp.float32)
    normed2 = normalize(resid, ln2_gain).astype(jnp.bfloat16)
    act = jax.nn.gelu(jnp.dot(normed2, ff_in, preferred_element_type=jnp.float32), approximate=False).astype(jnp.bfloat16)
    encoded = (resid + jnp.dot(act, ff_out, preferred_element_type=jnp.float32)).astype(jnp.bfloat16)
    encoded = jnp.where(valid[:, None], encoded, jnp.zeros_like(encoded))
    zed = jnp.dot(encoded, pool_weight, preferred_element_type=jnp.float32)
    hidden = pool_weight.shape[1] // 2
    gate = jnp.tanh(zed[:, :hidden]) * jax.nn.sigmoid(zed[:, hidden:])
    logits = jnp.dot(gate, class_weight, precision=lax.Precision.HIGHEST)
    logits = jnp.where(valid[:, None], logits, -1e+30)
    peak = lax.optimization_barrier(jnp.max(logits, axis=0))
    expo = jnp.exp(logits - peak[None, :]) * valid[:, None].astype(jnp.float32)
    numer = jnp.dot(expo.T, encoded.astype(jnp.float32), precision=lax.Precision.HIGHEST)
    pooled = numer / lax.optimization_barrier(jnp.sum(expo, axis=0))[:, None]
    return (encoded, pooled)

def reference(tiles, counts, ln1_gain, qkv_weight, out_weight, ln2_gain, ff_in, ff_out, pool_weight, class_weight):

    def run(item):
        return one_slide((item[0], item[1], ln1_gain, qkv_weight, out_weight, ln2_gain, ff_in, ff_out, pool_weight, class_weight))
    encoded, pooled = lax.map(run, (tiles, counts))
    return (encoded, pooled)
```

```python
import functools

import jax
import jax.numpy as jnp
from jax import lax
from jax.experimental import pallas as pl
from jax.experimental.pallas import tpu as pltpu
from jax.sharding import Mesh
from jax.sharding import PartitionSpec as P


HEADS = 16
BLOCK = 256
WIDE = 896
SEQ = ("seq_0", "seq_1", "seq_2")
F32 = jnp.float32
BF16 = jnp.bfloat16
LOG2E = 1.4426950408889634
LN2 = 0.6931471805599453


def dot(a, b):
    return jnp.dot(a, b, preferred_element_type=F32)


def dot_nt(a, b):
    return lax.dot_general(a, b, (((1,), (1,)), ((), ())), preferred_element_type=F32)


def norm_rows(x, gain):
    centre = jnp.mean(x, axis=-1, keepdims=True)
    c = x - centre
    spread = jnp.mean(c * c, axis=-1, keepdims=True)
    return c * lax.rsqrt(spread + 1e-05) * gain


def thirds(x):
    hi = x.astype(BF16).astype(F32)
    rest = x - hi
    mid = rest.astype(BF16).astype(F32)
    return hi, mid, (rest - mid).astype(BF16).astype(F32)


def attention(near, slide, here_ref, counts_ref, x_ref, gain_ref, w_ref, out_ref, nrm, qs, ks, vt, ot, lt):
    step = pl.program_id(0)
    here, count = here_ref[0], counts_ref[slide]
    rows, width = nrm.shape
    head_dim = width // HEADS
    half = HEADS // 2
    span = half * head_dim

    def place(index):
        if near:
            block, rest = index // 256, index % 256
            return here * rows + block * 256 + (rest % 8) * 32 + rest // 8
        return index * 32 + here

    @pl.when(step == 0)
    def _():
        x = x_ref[...].astype(F32)
        pos = place(lax.broadcasted_iota(jnp.int32, (rows, 1), 0))
        if near:
            x = jnp.concatenate(
                [x[:, 8 * b : 8 * b + 8].reshape(rows // 2, width) for b in range(2)], 0
            )
            first = jnp.concatenate(
                [jnp.broadcast_to(x[b * 256 : b * 256 + 1], (256, width)) for b in range(2)], 0
            )
        else:
            x = x.reshape(rows, width)
            first = jnp.broadcast_to(x[0:1], x.shape)
        x = jnp.where(pos < count, x, first)
        nrm[...] = norm_rows(x, gain_ref[...]).astype(BF16)
        qs[...] = dot(nrm[...], w_ref[...]).astype(BF16)

    @pl.when(step == 1)
    def _():
        ks[...] = dot(nrm[...], w_ref[...]).astype(BF16)

    @pl.when(step == 2)
    def _():
        v = dot(nrm[...], w_ref[...])
        live = place(lax.broadcasted_iota(jnp.int32, (1, rows), 1)) < count
        values = jnp.where(live, v.T, 0.0).astype(BF16)
        ones = jnp.where(
            lax.broadcasted_iota(jnp.int32, (16, rows), 0) == 0, jnp.where(live, 1.0, 0.0), 0.0
        ).astype(BF16)
        for h in range(HEADS):
            vt[h // half, h % half, :head_dim] = values[h * head_dim : (h + 1) * head_dim]
            vt[h // half, h % half, head_dim:] = ones
        scale = LOG2E / head_dim**0.5
        keys = BLOCK if near else rows

        def part(i, carry):
            g, t = i // 2, i % 2
            base = pl.multiple_of(g * span, 128)
            qrow = pl.multiple_of(t * 256, 256)
            krow = qrow if near else 0
            for hh in range(half):
                off = hh * head_dim
                w0 = off // 128 * 128
                wide = 128 if off + head_dim <= w0 + 128 else 256
                lane = lax.broadcasted_iota(jnp.int32, (1, wide), 1) + w0
                inside = jnp.where((lane >= off) & (lane < off + head_dim), 1.0, 0.0).astype(BF16)
                cols = pl.ds(base + w0, wide)
                kh = ks[pl.ds(krow, keys), cols] * inside
                s = dot_nt(kh, qs[pl.ds(qrow, 256), cols])
                m = jnp.max(s, axis=0, keepdims=True) * scale
                p = jnp.exp2(s * scale - m).astype(BF16)
                o = dot(vt[g, hh, :, pl.ds(krow, keys)], p)
                total = jnp.maximum(o[head_dim : head_dim + 1], 1e-30)
                ot[g, off : off + head_dim, pl.ds(qrow, 256)] = o[:head_dim] * (1.0 / total)
                lt[g, hh : hh + 1, pl.ds(qrow, 256)] = (m + jnp.log2(total)) * LN2
            return carry

        lax.fori_loop(0, 4, part, 0)
        out_ref[:, :width] = ot[...].reshape(width, rows).T.astype(out_ref.dtype)
        pieces = thirds(lt[...].reshape(HEADS, rows))
        tail = jnp.concatenate([*pieces, jnp.zeros((128 - 3 * HEADS, rows), F32)], 0)
        out_ref[:, width:] = tail.T.astype(out_ref.dtype)


def attend(near, slide, where, x, gain, weight):
    classes, _, tall, width = x.shape
    rows = classes * tall
    keys = BLOCK if near else rows
    dtype = F32 if near else BF16
    return pl.pallas_call(
        functools.partial(attention, near, slide),
        out_shape=jax.ShapeDtypeStruct((rows, WIDE), dtype),
        grid_spec=pltpu.PrefetchScalarGridSpec(
            num_scalar_prefetch=2,
            grid=(3,),
            in_specs=[
                pl.BlockSpec((classes, None, tall, width), lambda i, *_: (0, slide, 0, 0)),
                pl.BlockSpec((1, width), lambda i, *_: (0, 0)),
                pl.BlockSpec((width, width), lambda i, *_: (0, i)),
            ],
            out_specs=pl.BlockSpec((rows, WIDE), lambda i, *_: (0, 0)),
            scratch_shapes=[
                pltpu.VMEM((rows, width), BF16),
                pltpu.VMEM((rows, width), BF16),
                pltpu.VMEM((rows, width), BF16),
                pltpu.VMEM((2, HEADS // 2, width // HEADS + 16, rows), BF16),
                pltpu.VMEM((2, width // 2, rows), F32),
                pltpu.VMEM((2, HEADS // 2, rows), F32),
            ],
        ),
        cost_estimate=pl.CostEstimate(
            flops=2 * rows * width * (3 * width + 2 * keys),
            bytes_accessed=2 * 3 * width * width + 6 * rows * width,
            transcendentals=rows * keys * HEADS,
        ),
        name="near" if near else "far",
    )(*where, x, gain, weight)


def gelu(x):
    return 0.5 * x * (1.0 + lax.erf(x * 0.7071067811865476))


def post(
    slide,
    here_ref,
    counts_ref,
    grp_ref,
    x_ref,
    near_ref,
    far_ref,
    wo_ref,
    gain_ref,
    w1_ref,
    w2_ref,
    wp_ref,
    cw_ref,
    enc_ref,
    red_ref,
    encs,
    logit,
):
    step = pl.program_id(0)
    here, count = here_ref[0], counts_ref[slide]
    width = wo_ref.shape[0]
    head_dim = width // HEADS
    rows = near_ref.shape[0]
    far = far_ref[...].astype(F32).reshape(rows, WIDE)
    near = near_ref[...]
    row = lax.broadcasted_iota(jnp.int32, (256, width), 0)
    lane = lax.broadcasted_iota(jnp.int32, (256, width), 1)
    slot = row % 128
    head = slot % HEADS
    hit = (slot < 3 * HEADS) & (lane >= head * head_dim) & (lane < head * head_dim + head_dim)
    spread = jnp.where(hit, jnp.where(row < 128, 1.0, -1.0), 0.0).astype(BF16)
    parts = jnp.concatenate([near[:, width:], far[:, width:]], 1).astype(BF16)
    gap = dot(parts, spread)
    share = 1.0 / (1.0 + jnp.exp(-gap))
    mixed = (share * near[:, :width] + (1.0 - share) * far[:, :width]).astype(BF16)
    resid = x_ref[...].astype(F32).reshape(rows, width) + dot(mixed, wo_ref[...])
    n2 = norm_rows(resid, gain_ref[...]).astype(BF16)
    acc = resid
    chunk = 512
    for f in range(w1_ref.shape[1] // chunk):
        u = dot(n2, w1_ref[:, f * chunk : (f + 1) * chunk])
        acc = acc + dot(gelu(u).astype(BF16), w2_ref[f * chunk : (f + 1) * chunk, :])

    def place(index):
        return here * 512 + step * 256 + (index % 8) * 32 + index // 8

    live = place(lax.broadcasted_iota(jnp.int32, (rows, 1), 0)) < count
    enc32 = jnp.where(live, acc, 0.0).astype(BF16).astype(F32)
    enc = enc32.astype(BF16)
    enc_ref[...] = enc32.reshape(enc_ref.shape).astype(BF16)
    at = pl.multiple_of(step * rows, 256)
    encs[pl.ds(at, rows), :] = enc
    pool = [wp_ref[lax.rem(grp_ref[0] - k + 4, 4)] for k in range(4)]
    z = dot(enc, jnp.concatenate(pool, 0))
    hidden = width // 2
    gate = jnp.tanh(z[:, :hidden]) * (1.0 / (1.0 + jnp.exp(-z[:, hidden:])))
    g_hi, g_mid, g_lo = thirds(gate)
    cw = cw_ref[...]
    c_hi, c_mid, c_lo = thirds(cw)
    stack = jnp.concatenate([c_hi, c_mid, c_lo], 0).astype(BF16)
    one = dot_nt(stack, g_hi.astype(BF16))
    two = dot_nt(stack[:16], g_mid.astype(BF16))
    three = dot_nt(stack[:16], g_lo.astype(BF16))
    logits = one[0:8] + ((one[8:16] + two[0:8]) + (one[16:24] + two[8:16] + three[0:8]))
    live_t = place(lax.broadcasted_iota(jnp.int32, (1, rows), 1)) < count
    logit[:, pl.ds(at, rows)] = jnp.where(live_t, logits, -1e30)

    @pl.when(step == 1)
    def _():
        every = logit[...]
        peak = jnp.max(every, axis=1, keepdims=True)
        e = jnp.where(every > -1e29, jnp.exp(every - peak), 0.0)
        total = jnp.sum(e, axis=1, keepdims=True)
        pieces = jnp.concatenate(thirds(e), 0).astype(BF16)
        numer = dot(pieces, encs[...])
        red_ref[:, :width] = numer[0:8] + (numer[8:16] + numer[16:24])
        red_ref[:, width : width + 128] = jnp.broadcast_to(peak, (8, 128))
        red_ref[:, width + 128 :] = jnp.broadcast_to(total, (8, 128))


def finish(slide, where, x, near, back, wo, gain, w1, w2, wp, cw):
    classes, _, tall, width = x.shape
    rows = classes * tall
    hidden = w1.shape[1]
    once = pl.Buffered(1)
    return pl.pallas_call(
        functools.partial(post, slide),
        out_shape=(
            jax.ShapeDtypeStruct((classes, tall, width), BF16),
            jax.ShapeDtypeStruct((8, width + 256), F32),
        ),
        grid_spec=pltpu.PrefetchScalarGridSpec(
            num_scalar_prefetch=3,
            grid=(2,),
            in_specs=[
                pl.BlockSpec((classes, None, 8, width), lambda i, *_: (0, slide, i, 0)),
                pl.BlockSpec((rows // 2, WIDE), lambda i, *_: (i, 0)),
                pl.BlockSpec((classes, 8, WIDE), lambda i, *_: (0, i, 0)),
                pl.BlockSpec((width, width), lambda i, *_: (0, 0), pipeline_mode=once),
                pl.BlockSpec((1, width), lambda i, *_: (0, 0)),
                pl.BlockSpec((width, hidden), lambda i, *_: (0, 0), pipeline_mode=once),
                pl.BlockSpec((hidden, width), lambda i, *_: (0, 0), pipeline_mode=once),
                pl.BlockSpec((4, width // 4, width), lambda i, *_: (0, 0, 0), pipeline_mode=once),
                pl.BlockSpec((8, width // 2), lambda i, *_: (0, 0)),
            ],
            out_specs=(
                pl.BlockSpec((classes, 8, width), lambda i, *_: (0, i, 0)),
                pl.BlockSpec((8, width + 256), lambda i, *_: (0, 0)),
            ),
            scratch_shapes=[pltpu.VMEM((rows, width), BF16), pltpu.VMEM((8, rows), F32)],
        ),
        cost_estimate=pl.CostEstimate(
            flops=2 * rows * width * (2 * width + 2 * hidden),
            bytes_accessed=4 * width * (width + hidden) + 8 * rows * width,
            transcendentals=rows * hidden,
        ),
        name="post",
    )(*where, x, near, back, wo, gain, w1, w2, wp, cw)


def fold(last, *refs):
    *pieces, out_ref = refs
    width = 768
    peaks = [p[:, width : width + 128] for p in pieces]
    top = functools.reduce(jnp.maximum, peaks)
    numer, total = 0.0, 0.0
    for p, peak in zip(pieces, peaks):
        w = jnp.exp(peak - top)
        numer = numer + p[:, :width] * jnp.concatenate([w] * 6, 1)
        total = total + p[:, width + 128 :] * w
    if last:
        out_ref[...] = numer / jnp.concatenate([total] * 6, 1)
    else:
        out_ref[:, :width] = numer
        out_ref[:, width : width + 128] = top
        out_ref[:, width + 128 :] = total


def folded(pieces, last):
    rows, wide = pieces[0].shape
    return pl.pallas_call(
        functools.partial(fold, last),
        out_shape=jax.ShapeDtypeStruct((rows, 768 if last else wide), F32),
        name="fold",
    )(*pieces)


def joined(x, axes):
    for axis in axes:
        size = lax.axis_size(axis)
        pieces = [x] + [
            lax.ppermute(x, axis, [(i, (i + k) % size) for i in range(size)])
            for k in range(1, size)
        ]
        x = folded(pieces, axis == axes[-1])
    return x


def exchange(x):
    return lax.all_to_all(x, SEQ, 0, 0, tiled=True)


def layer(
    tiles,
    counts,
    ln1_gain,
    qkv_weight,
    out_weight,
    ln2_gain,
    ff_in,
    ff_out,
    pool_weight,
    class_weight,
):
    slides, rows, width = tiles.shape
    ratio = lax.axis_size(SEQ)
    here = lax.axis_index(SEQ)
    where = (here.astype(jnp.int32).reshape(1), counts)
    gain1, gain2 = ln1_gain.reshape(1, width), ln2_gain.reshape(1, width)
    mine = jnp.transpose(
        tiles.reshape(slides, rows // ratio, ratio, width), (2, 0, 1, 3)
    )
    moved = exchange(mine)
    mine_at = lax.axis_index("grp")
    quarters = [pool_weight] + [
        lax.ppermute(pool_weight, "grp", [(i, (i + k) % 4) for i in range(4)]) for k in (1, 2, 3)
    ]
    whole = jnp.stack(quarters)
    near = []
    for s in range(slides):
        near.append(attend(True, s, where, mine, gain1, qkv_weight))
    back = []
    for s in range(slides):
        far = attend(False, s, where, moved, gain1, qkv_weight)
        back.append(exchange(far.reshape(ratio, rows // ratio, WIDE)))
    encoded, partial = [], []
    for s in range(slides):
        enc, red = finish(
            s, (*where, mine_at.astype(jnp.int32).reshape(1)), mine, near[s], back[s], out_weight, gain2, ff_in, ff_out, whole,
            class_weight.T,
        )
        encoded.append(jnp.swapaxes(enc, 0, 1).reshape(rows, width))
        partial.append(red)
    pooled = joined(jnp.concatenate(partial, 0), SEQ[::-1])
    return (jnp.stack(encoded), pooled.reshape(slides, 8, width))


def solution(mesh):
    torus = Mesh(
        mesh.devices.reshape(mesh.shape["grp"], 4, 4, 2), ("grp", "seq_0", "seq_1", "seq_2")
    )
    return jax.shard_map(
        layer,
        mesh=torus,
        in_specs=(P("grp", SEQ, None), P("grp"), P(), P(), P(), P(), P(), P(), P("grp", None), P()),
        out_specs=(P("grp", SEQ, None), P("grp", None, None)),
        check_vma=False,
    )
```

```python
import functools

import jax
import jax.numpy as jnp
from jax import lax
from jax.experimental import pallas as pl
from jax.experimental.pallas import tpu as pltpu
from jax.sharding import Mesh
from jax.sharding import PartitionSpec as P


HEADS = 16
BLOCK = 256
WIDE = 896
SEQ = ("seq_0", "seq_1", "seq_2")
F32 = jnp.float32
BF16 = jnp.bfloat16
LOG2E = 1.4426950408889634
LN2 = 0.6931471805599453


def dot(a, b):
    return jnp.dot(a, b, preferred_element_type=F32)


def dot_nt(a, b):
    return lax.dot_general(a, b, (((1,), (1,)), ((), ())), preferred_element_type=F32)


def norm_rows(x, gain):
    centre = jnp.mean(x, axis=-1, keepdims=True)
    c = x - centre
    spread = jnp.mean(c * c, axis=-1, keepdims=True)
    return c * lax.rsqrt(spread + 1e-05) * gain


def thirds(x):
    hi = x.astype(BF16).astype(F32)
    rest = x - hi
    mid = rest.astype(BF16).astype(F32)
    return hi, mid, (rest - mid).astype(BF16).astype(F32)


def attention(near, slide, here_ref, counts_ref, x_ref, gain_ref, w_ref, out_ref, nrm, qs, ks, vt, ot, lt, sc, mx, ps):
    step = pl.program_id(0)
    here, count = here_ref[0], counts_ref[slide]
    rows, width = nrm.shape
    head_dim = width // HEADS
    half = HEADS // 2
    span = half * head_dim

    def place(index):
        if near:
            block, rest = index // 256, index % 256
            return here * rows + block * 256 + (rest % 8) * 32 + rest // 8
        return index * 32 + here

    @pl.when(step == 0)
    def _():
        x = x_ref[...].astype(F32)
        pos = place(lax.broadcasted_iota(jnp.int32, (rows, 1), 0))
        if near:
            x = jnp.concatenate(
                [x[:, 8 * b : 8 * b + 8].reshape(rows // 2, width) for b in range(2)], 0
            )
            first = jnp.concatenate(
                [jnp.broadcast_to(x[b * 256 : b * 256 + 1], (256, width)) for b in range(2)], 0
            )
        else:
            x = x.reshape(rows, width)
            first = jnp.broadcast_to(x[0:1], x.shape)
        x = jnp.where(pos < count, x, first)
        nrm[...] = norm_rows(x, gain_ref[...]).astype(BF16)
        qs[...] = dot(nrm[...], w_ref[...]).astype(BF16)

    @pl.when(step == 1)
    def _():
        ks[...] = dot(nrm[...], w_ref[...]).astype(BF16)

    @pl.when(step == 2)
    def _():
        v = dot(nrm[...], w_ref[...])
        live = place(lax.broadcasted_iota(jnp.int32, (1, rows), 1)) < count
        values = jnp.where(live, v.T, 0.0).astype(BF16)
        ones = jnp.where(
            lax.broadcasted_iota(jnp.int32, (16, rows), 0) == 0, jnp.where(live, 1.0, 0.0), 0.0
        ).astype(BF16)
        for h in range(HEADS):
            vt[h // half, h % half, :head_dim] = values[h * head_dim : (h + 1) * head_dim]
            vt[h // half, h % half, head_dim:] = ones
        scale = LOG2E / head_dim**0.5
        keys = BLOCK if near else rows

        def corner(i):
            g, t = i // 2, i % 2
            qrow = pl.multiple_of(t * 256, 256)
            return g, pl.multiple_of(g * span, 128), qrow, qrow if near else 0

        def scores(i, hh):
            _, base, qrow, krow = corner(i)
            off = hh * head_dim
            w0 = off // 128 * 128
            wide = 128 if off + head_dim <= w0 + 128 else 256
            lane = lax.broadcasted_iota(jnp.int32, (1, wide), 1) + w0
            inside = jnp.where((lane >= off) & (lane < off + head_dim), 1.0, 0.0).astype(BF16)
            cols = pl.ds(base + w0, wide)
            kh = ks[pl.ds(krow, keys), cols] * inside
            s = dot_nt(kh, qs[pl.ds(qrow, 256), cols])
            sc[hh % 2] = s
            mx[hh % 4] = jnp.max(s, axis=0, keepdims=True) * scale

        def weights(hh):
            s = sc[hh % 2]
            ps[hh % 2] = jnp.exp2(s * scale - mx[hh % 4]).astype(BF16)

        def mix(i, hh):
            g, _, qrow, krow = corner(i)
            off = hh * head_dim
            o = dot(vt[g, hh, :, pl.ds(krow, keys)], ps[hh % 2])
            total = jnp.maximum(o[head_dim : head_dim + 1], 1e-30)
            ot[g, off : off + head_dim, pl.ds(qrow, 256)] = o[:head_dim] * (1.0 / total)
            lt[g, hh : hh + 1, pl.ds(qrow, 256)] = (mx[hh % 4] + jnp.log2(total)) * LN2

        def part(i, carry):
            for hh in range(half):
                if hh + 1 < half:
                    scores(i, hh + 1)
                else:
                    scores(lax.rem(i + 1, 4), 0)
                if hh:
                    mix(i, hh - 1)
                else:
                    mix(lax.rem(i + 3, 4), half - 1)
                weights(hh)
            return carry

        scores(0, 0)
        lax.fori_loop(0, 4, part, 0)
        mix(3, half - 1)
        out_ref[:, :width] = ot[...].reshape(width, rows).T.astype(out_ref.dtype)
        pieces = thirds(lt[...].reshape(HEADS, rows))
        tail = jnp.concatenate([*pieces, jnp.zeros((128 - 3 * HEADS, rows), F32)], 0)
        out_ref[:, width:] = tail.T.astype(out_ref.dtype)


def attend(near, slide, where, x, gain, weight):
    classes, _, tall, width = x.shape
    rows = classes * tall
    keys = BLOCK if near else rows
    dtype = F32 if near else BF16
    return pl.pallas_call(
        functools.partial(attention, near, slide),
        out_shape=pltpu.HBM((rows, WIDE), dtype),
        grid_spec=pltpu.PrefetchScalarGridSpec(
            num_scalar_prefetch=2,
            grid=(3,),
            in_specs=[
                pl.BlockSpec((classes, None, tall, width), lambda i, *_: (0, slide, 0, 0)),
                pl.BlockSpec((1, width), lambda i, *_: (0, 0)),
                pl.BlockSpec((width, width), lambda i, *_: (0, i)),
            ],
            out_specs=pl.BlockSpec((rows, WIDE), lambda i, *_: (0, 0)),
            scratch_shapes=[
                pltpu.VMEM((rows, width), BF16),
                pltpu.VMEM((rows, width), BF16),
                pltpu.VMEM((rows, width), BF16),
                pltpu.VMEM((2, HEADS // 2, width // HEADS + 16, rows), BF16),
                pltpu.VMEM((2, width // 2, rows), F32),
                pltpu.VMEM((2, HEADS // 2, rows), F32),
                pltpu.VMEM((2, keys, 256), F32),
                pltpu.VMEM((4, 1, 256), F32),
                pltpu.VMEM((2, keys, 256), BF16),
            ],
        ),
        compiler_params=pltpu.CompilerParams(vmem_limit_bytes=20 << 20),
        cost_estimate=pl.CostEstimate(
            flops=2 * rows * width * (3 * width + 2 * keys),
            bytes_accessed=2 * 3 * width * width + 6 * rows * width,
            transcendentals=rows * keys * HEADS,
        ),
        name="near" if near else "far",
    )(*where, x, gain, weight)


def gelu(x):
    return 0.5 * x * (1.0 + lax.erf(x * 0.7071067811865476))


def halves(x):
    return jnp.concatenate([x[:, 8 * b : 8 * b + 8].reshape(256, x.shape[2]) for b in range(2)], 0)


def post(slide, here_ref, counts_ref, grp_ref, *refs):
    x_ref, near_ref, far_ref, wo_ref, gain_ref, w1_ref, w2_ref, *refs = refs
    *wp_refs, cw_ref = refs[:5]
    refs = refs[5:]
    if slide:
        other_ref, *refs = refs
    enc_ref, red_ref, n2s, acc, encs, logit, w1, w2, pool, sem = refs
    step = pl.program_id(0)
    here, count = here_ref[0], counts_ref[slide]
    width = wo_ref.shape[0]
    head_dim = width // HEADS
    rows = near_ref.shape[0]
    fetch = [pltpu.make_async_copy(w1_ref, w1, sem.at[4]), pltpu.make_async_copy(w2_ref, w2, sem.at[5])] + [
        pltpu.make_async_copy(wp_refs[k], pool.at[lax.rem(grp_ref[0] - k + 4, 4)], sem.at[k])
        for k in range(4)
    ]

    @pl.when(step == 0)
    def _():
        for copy in fetch:
            copy.start()
        far = halves(far_ref[...].astype(F32))
        near = near_ref[...]
        row = lax.broadcasted_iota(jnp.int32, (256, width), 0)
        lane = lax.broadcasted_iota(jnp.int32, (256, width), 1)
        slot = row % 128
        head = slot % HEADS
        hit = (slot < 3 * HEADS) & (lane >= head * head_dim) & (lane < head * head_dim + head_dim)
        spread = jnp.where(hit, jnp.where(row < 128, 1.0, -1.0), 0.0).astype(BF16)
        parts = jnp.concatenate([near[:, width:], far[:, width:]], 1).astype(BF16)
        gap = dot(parts, spread)
        share = 1.0 / (1.0 + jnp.exp(-gap))
        mixed = (share * near[:, :width] + (1.0 - share) * far[:, :width]).astype(BF16)
        resid = halves(x_ref[...].astype(F32)) + dot(mixed, wo_ref[...])
        acc[...] = resid
        n2s[...] = norm_rows(resid, gain_ref[...]).astype(BF16)
        for copy in fetch:
            copy.wait()

    @pl.when(step > 0)
    def _():
        at = pl.multiple_of((step - 1) * 256, 256)

        def place(index):
            return here * rows + at + (index % 8) * 32 + index // 8

        n2 = n2s[pl.ds(at, 256), :]
        total = acc[pl.ds(at, 256), :]
        chunk = 512
        hidden = w1.shape[1]
        ahead = dot(n2, w1[:, :chunk])
        for f in range(hidden // chunk):
            u = ahead
            if (f + 1) * chunk < hidden:
                ahead = dot(n2, w1[:, (f + 1) * chunk : (f + 2) * chunk])
            total = total + dot(gelu(u).astype(BF16), w2[f * chunk : (f + 1) * chunk, :])
        live = place(lax.broadcasted_iota(jnp.int32, (256, 1), 0)) < count
        enc32 = jnp.where(live, total, 0.0).astype(BF16).astype(F32)
        enc = enc32.astype(BF16)
        enc_ref[...] = enc32.reshape(enc_ref.shape).astype(BF16)
        encs[pl.ds(at, 256), :] = enc
        z = dot(enc, pool[...].reshape(width, width))
        hidden = width // 2
        gate = jnp.tanh(z[:, :hidden]) * (1.0 / (1.0 + jnp.exp(-z[:, hidden:])))
        g_hi, g_mid, g_lo = thirds(gate)
        stack = jnp.concatenate(thirds(cw_ref[...]), 0).astype(BF16)
        one = dot_nt(stack, g_hi.astype(BF16))
        two = dot_nt(stack[:16], g_mid.astype(BF16))
        three = dot_nt(stack[:16], g_lo.astype(BF16))
        logits = one[0:8] + ((one[8:16] + two[0:8]) + (one[16:24] + two[8:16] + three[0:8]))
        live_t = place(lax.broadcasted_iota(jnp.int32, (1, 256), 1)) < count
        logit[:, pl.ds(at, 256)] = jnp.where(live_t, logits, -1e30)

    @pl.when(step == 2)
    def _():
        every = logit[...]
        peak = jnp.max(every, axis=1, keepdims=True)
        e = jnp.where(every > -1e29, jnp.exp(every - peak), 0.0)
        total = jnp.sum(e, axis=1, keepdims=True)
        numer = dot(jnp.concatenate(thirds(e), 0).astype(BF16), encs[...])
        numer = numer[0:8] + (numer[8:16] + numer[16:24])
        tail = jnp.zeros((8, 128), F32)
        at = lax.broadcasted_iota(jnp.int32, (8, 128), 1)
        for k, piece in enumerate((*thirds(peak), *thirds(total))):
            tail = jnp.where(at == k, piece, tail)
        mine = jnp.concatenate([numer, tail], 1)
        if slide:
            both = jnp.concatenate([other_ref[...], mine], 0).astype(BF16)
            red_ref[...] = jnp.broadcast_to(both[None], red_ref.shape)
        else:
            red_ref[...] = mine


def finish(slide, where, x, near, back, wo, gain, w1, w2, wp, cw, other=None):
    classes, _, tall, width = x.shape
    rows = classes * tall
    hidden = w1.shape[1]
    once = pl.Buffered(1)
    if slide:
        red = pltpu.HBM((classes, 16, WIDE), BF16)
    else:
        red = pltpu.HBM((8, WIDE), F32)
    extra = [pl.BlockSpec((8, WIDE), lambda i, *_: (0, 0))] if slide else []
    return pl.pallas_call(
        functools.partial(post, slide),
        out_shape=(pltpu.HBM((classes, tall, width), BF16), red),
        grid_spec=pltpu.PrefetchScalarGridSpec(
            num_scalar_prefetch=3,
            grid=(3,),
            in_specs=[
                pl.BlockSpec(
                    (classes, None, tall, width), lambda i, *_: (0, slide, 0, 0), pipeline_mode=once
                ),
                pl.BlockSpec((rows, WIDE), lambda i, *_: (0, 0), pipeline_mode=once),
                pl.BlockSpec((classes, tall, WIDE), lambda i, *_: (0, 0, 0), pipeline_mode=once),
                pl.BlockSpec((width, width), lambda i, *_: (0, 0), pipeline_mode=once),
                pl.BlockSpec((1, width), lambda i, *_: (0, 0)),
                *[pl.BlockSpec(memory_space=pltpu.HBM)] * 6,
                pl.BlockSpec((8, width // 2), lambda i, *_: (0, 0)),
                *extra,
            ],
            out_specs=(
                pl.BlockSpec((classes, 8, width), lambda i, *_: (0, jnp.maximum(i - 1, 0), 0)),
                pl.BlockSpec(red.shape, lambda i, *_: (0,) * len(red.shape)),
            ),
            scratch_shapes=[
                pltpu.VMEM((rows, width), BF16),
                pltpu.VMEM((rows, width), F32),
                pltpu.VMEM((rows, width), BF16),
                pltpu.VMEM((8, rows), F32),
                pltpu.VMEM((width, hidden), BF16),
                pltpu.VMEM((hidden, width), BF16),
                pltpu.VMEM((4, width // 4, width), BF16),
                pltpu.SemaphoreType.DMA((6,)),
            ],
        ),
        compiler_params=pltpu.CompilerParams(vmem_limit_bytes=34 << 20),
        cost_estimate=pl.CostEstimate(
            flops=2 * rows * width * (2 * width + 2 * hidden),
            bytes_accessed=4 * width * (width + hidden) + 8 * rows * width,
            transcendentals=rows * hidden,
        ),
        name="post",
    )(*where, x, near, back, wo, gain, w1, w2, *wp, cw, *([other] if slide else []))


def fold(x_ref, out_ref):
    width = out_ref.shape[1]
    tail = x_ref[:, :, width:].astype(F32)
    at = lax.broadcasted_iota(jnp.int32, tail.shape, 2)
    peak = jnp.sum(jnp.where(at < 3, tail, 0.0), axis=2, keepdims=True)
    total = jnp.sum(jnp.where((at >= 3) & (at < 6), tail, 0.0), axis=2, keepdims=True)
    w = jnp.exp(peak - jnp.max(peak, axis=0, keepdims=True))
    numer = jnp.sum(w * x_ref[:, :, :width].astype(F32), axis=0)
    out_ref[...] = numer / jnp.sum(w * total, axis=0)


def joined(x):
    rows = x.shape[1]
    return pl.pallas_call(
        fold,
        out_shape=jax.ShapeDtypeStruct((rows, x.shape[2] - 128), F32),
        compiler_params=pltpu.CompilerParams(vmem_limit_bytes=16 << 20),
        name="fold",
    )(exchange(x))


def exchange(x):
    return lax.all_to_all(x, SEQ, 0, 0, tiled=True)


def layer(
    tiles,
    counts,
    ln1_gain,
    qkv_weight,
    out_weight,
    ln2_gain,
    ff_in,
    ff_out,
    pool_weight,
    class_weight,
):
    slides, rows, width = tiles.shape
    ratio = lax.axis_size(SEQ)
    here = lax.axis_index(SEQ)
    where = (here.astype(jnp.int32).reshape(1), counts)
    gain1, gain2 = ln1_gain.reshape(1, width), ln2_gain.reshape(1, width)
    mine = jnp.transpose(
        tiles.reshape(slides, rows // ratio, ratio, width), (2, 0, 1, 3)
    )
    moved = exchange(mine)
    mine_at = lax.axis_index("grp")
    quarters = [pool_weight]
    for k in (1, 2, 3):
        quarters.append(lax.ppermute(pool_weight, "grp", [(i, (i + k) % 4) for i in range(4)]))
    whole = [pltpu.with_memory_space_constraint(q, pltpu.HBM) for q in quarters]
    qkv_weight, out_weight, ff_in, ff_out = (
        pltpu.with_memory_space_constraint(w, pltpu.HBM)
        for w in (qkv_weight, out_weight, ff_in, ff_out)
    )
    near = []
    for s in range(slides):
        out = attend(True, s, where, mine, gain1, qkv_weight)
        near.append(pltpu.with_memory_space_constraint(out, pltpu.HBM))
    back = []
    for s in range(slides):
        far = attend(False, s, where, moved, gain1, qkv_weight)
        back.append(exchange(far.reshape(ratio, rows // ratio, WIDE)))
    encoded, partial = [], []
    for s in range(slides):
        enc, red = finish(
            s, (*where, mine_at.astype(jnp.int32).reshape(1)), mine, near[s], back[s], out_weight, gain2, ff_in, ff_out, whole,
            class_weight.T, *partial,
        )
        encoded.append(jnp.swapaxes(enc, 0, 1).reshape(rows, width))
        partial.append(red if s else pltpu.with_memory_space_constraint(red, pltpu.HBM))
    pooled = joined(partial[1])
    return (jnp.stack(encoded), pooled.reshape(slides, 8, width))


def solution(mesh):
    torus = Mesh(
        mesh.devices.reshape(mesh.shape["grp"], 4, 4, 2), ("grp", "seq_0", "seq_1", "seq_2")
    )
    return jax.shard_map(
        layer,
        mesh=torus,
        in_specs=(P("grp", SEQ, None), P("grp"), P(), P(), P(), P(), P(), P(), P("grp", None), P()),
        out_specs=(P("grp", SEQ, None), P("grp", None, None)),
        check_vma=False,
    )
```

```python
import functools

import jax
import jax.numpy as jnp
from jax import lax
from jax.experimental import pallas as pl
from jax.experimental.pallas import tpu as pltpu
from jax.sharding import Mesh
from jax.sharding import PartitionSpec as P


HEADS = 16
BLOCK = 256
WIDE = 896
SEQ = ("seq_0", "seq_1", "seq_2")
F32 = jnp.float32
BF16 = jnp.bfloat16
LOG2E = 1.4426950408889634
LN2 = 0.6931471805599453


def dot(a, b):
    return jnp.dot(a, b, preferred_element_type=F32)


def dot_nt(a, b):
    return lax.dot_general(a, b, (((1,), (1,)), ((), ())), preferred_element_type=F32)


def norm_rows(x, gain):
    centre = jnp.mean(x, axis=-1, keepdims=True)
    c = x - centre
    spread = jnp.mean(c * c, axis=-1, keepdims=True)
    return c * lax.rsqrt(spread + 1e-05) * gain


def thirds(x):
    hi = x.astype(BF16).astype(F32)
    rest = x - hi
    mid = rest.astype(BF16).astype(F32)
    return hi, mid, (rest - mid).astype(BF16).astype(F32)


def attention(near, slide, here_ref, counts_ref, x_ref, gain_ref, w_ref, out_ref, nrm, qs, ks, vt, ot, lt, sc, mx, ps):
    step = pl.program_id(0)
    here, count = here_ref[0], counts_ref[slide]
    rows, width = nrm.shape
    head_dim = width // HEADS
    half = HEADS // 2
    span = half * head_dim

    def place(index):
        if near:
            block, rest = index // 256, index % 256
            return here * rows + block * 256 + (rest % 8) * 32 + rest // 8
        return index * 32 + here

    @pl.when(step == 0)
    def _():
        x = x_ref[...].astype(F32)
        pos = place(lax.broadcasted_iota(jnp.int32, (rows, 1), 0))
        if near:
            x = jnp.concatenate(
                [x[:, 8 * b : 8 * b + 8].reshape(rows // 2, width) for b in range(2)], 0
            )
            first = jnp.concatenate(
                [jnp.broadcast_to(x[b * 256 : b * 256 + 1], (256, width)) for b in range(2)], 0
            )
        else:
            x = x.reshape(rows, width)
            first = jnp.broadcast_to(x[0:1], x.shape)
        x = jnp.where(pos < count, x, first)
        nrm[...] = norm_rows(x, gain_ref[...]).astype(BF16)
        qs[...] = dot(nrm[...], w_ref[...]).astype(BF16)

    @pl.when(step == 1)
    def _():
        ks[...] = dot(nrm[...], w_ref[...]).astype(BF16)

    @pl.when(step == 2)
    def _():
        v = dot(nrm[...], w_ref[...])
        live = place(lax.broadcasted_iota(jnp.int32, (1, rows), 1)) < count
        values = jnp.where(live, v.T, 0.0).astype(BF16)
        ones = jnp.where(
            lax.broadcasted_iota(jnp.int32, (16, rows), 0) == 0, jnp.where(live, 1.0, 0.0), 0.0
        ).astype(BF16)
        for h in range(HEADS):
            vt[h // half, h % half, :head_dim] = values[h * head_dim : (h + 1) * head_dim]
            vt[h // half, h % half, head_dim:] = ones
        scale = LOG2E / head_dim**0.5
        keys = BLOCK if near else rows

        def corner(i):
            g, t = i // 2, i % 2
            qrow = pl.multiple_of(t * 256, 256)
            return g, pl.multiple_of(g * span, 128), qrow, qrow if near else 0

        def scores(i, hh):
            _, base, qrow, krow = corner(i)
            off = hh * head_dim
            w0 = off // 128 * 128
            wide = 128 if off + head_dim <= w0 + 128 else 256
            lane = lax.broadcasted_iota(jnp.int32, (1, wide), 1) + w0
            inside = jnp.where((lane >= off) & (lane < off + head_dim), 1.0, 0.0).astype(BF16)
            cols = pl.ds(base + w0, wide)
            kh = ks[pl.ds(krow, keys), cols] * inside
            s = dot_nt(kh, qs[pl.ds(qrow, 256), cols])
            sc[hh % 2] = s
            mx[hh % 4] = jnp.max(s, axis=0, keepdims=True) * scale

        def weights(hh):
            s = sc[hh % 2]
            ps[hh % 2] = jnp.exp2(s * scale - mx[hh % 4]).astype(BF16)

        def mix(i, hh):
            g, _, qrow, krow = corner(i)
            off = hh * head_dim
            o = dot(vt[g, hh, :, pl.ds(krow, keys)], ps[hh % 2])
            total = jnp.maximum(o[head_dim : head_dim + 1], 1e-30)
            ot[g, off : off + head_dim, pl.ds(qrow, 256)] = o[:head_dim] * (1.0 / total)
            lt[g, hh : hh + 1, pl.ds(qrow, 256)] = (mx[hh % 4] + jnp.log2(total)) * LN2

        def part(i, carry):
            for hh in range(half):
                if hh + 1 < half:
                    scores(i, hh + 1)
                else:
                    scores(lax.rem(i + 1, 4), 0)
                if hh:
                    mix(i, hh - 1)
                else:
                    mix(lax.rem(i + 3, 4), half - 1)
                weights(hh)
            return carry

        scores(0, 0)
        lax.fori_loop(0, 4, part, 0)
        mix(3, half - 1)
        out_ref[:, :width] = ot[...].reshape(width, rows).T.astype(out_ref.dtype)
        pieces = thirds(lt[...].reshape(HEADS, rows))
        tail = jnp.concatenate([*pieces, jnp.zeros((128 - 3 * HEADS, rows), F32)], 0)
        out_ref[:, width:] = tail.T.astype(out_ref.dtype)


def attend(near, slide, where, x, gain, weight):
    classes, _, tall, width = x.shape
    rows = classes * tall
    keys = BLOCK if near else rows
    return pl.pallas_call(
        functools.partial(attention, near, slide),
        out_shape=pltpu.HBM((rows, WIDE), F32 if near else BF16),
        grid_spec=pltpu.PrefetchScalarGridSpec(
            num_scalar_prefetch=2,
            grid=(3,),
            in_specs=[
                pl.BlockSpec((classes, None, tall, width), lambda i, *_: (0, slide, 0, 0)),
                pl.BlockSpec((1, width), lambda i, *_: (0, 0)),
                pl.BlockSpec((width, width), lambda i, *_: (0, i)),
            ],
            out_specs=pl.BlockSpec((rows, WIDE), lambda i, *_: (0, 0)),
            scratch_shapes=[
                pltpu.VMEM((rows, width), BF16),
                pltpu.VMEM((rows, width), BF16),
                pltpu.VMEM((rows, width), BF16),
                pltpu.VMEM((2, HEADS // 2, width // HEADS + 16, rows), BF16),
                pltpu.VMEM((2, width // 2, rows), F32),
                pltpu.VMEM((2, HEADS // 2, rows), F32),
                pltpu.VMEM((2, keys, 256), F32),
                pltpu.VMEM((4, 1, 256), F32),
                pltpu.VMEM((2, keys, 256), BF16),
            ],
        ),
        compiler_params=pltpu.CompilerParams(vmem_limit_bytes=20 << 20),
        cost_estimate=pl.CostEstimate(
            flops=2 * rows * width * (3 * width + 2 * keys),
            bytes_accessed=2 * 3 * width * width + 6 * rows * width,
            transcendentals=rows * keys * HEADS,
        ),
        name="near" if near else "far",
    )(*where, x, gain, weight)


def gelu(x):
    return 0.5 * x * (1.0 + lax.erf(x * 0.7071067811865476))


def halves(x):
    return jnp.concatenate([x[:, 8 * b : 8 * b + 8].reshape(256, x.shape[2]) for b in range(2)], 0)


def post(slide, here_ref, counts_ref, grp_ref, core_ref, *refs):
    x_ref, near_ref, far_ref, wo_ref, gain_ref, w1_ref, w2_ref, *refs = refs
    *wp_refs, cw_ref = refs[:5]
    refs = refs[5:]
    if slide:
        other_ref, *refs = refs
    enc_ref, red_ref, n2s, acc, encs, us, logit, w1, w2, pool, sem = refs
    step = pl.program_id(0)
    here, count = here_ref[0], counts_ref[slide]
    width = wo_ref.shape[0]
    head_dim = width // HEADS
    rows = near_ref.shape[0]
    fetch = [pltpu.make_async_copy(w1_ref, w1, sem.at[4]), pltpu.make_async_copy(w2_ref, w2, sem.at[5])] + [
        pltpu.make_async_copy(wp_refs[k], pool.at[lax.rem(grp_ref[0] - k + 4, 4)], sem.at[k])
        for k in range(4)
    ]

    @pl.when(step == 0)
    def _():
        for copy in fetch:
            copy.start()
        far = halves(far_ref[...].astype(F32))
        near = near_ref[...].astype(F32)
        row = lax.broadcasted_iota(jnp.int32, (256, width), 0)
        lane = lax.broadcasted_iota(jnp.int32, (256, width), 1)
        slot = row % 128
        head = slot % HEADS
        hit = (slot < 3 * HEADS) & (lane >= head * head_dim) & (lane < head * head_dim + head_dim)
        spread = jnp.where(hit, jnp.where(row < 128, 1.0, -1.0), 0.0).astype(BF16)
        parts = jnp.concatenate([near[:, width:], far[:, width:]], 1).astype(BF16)
        gap = dot(parts, spread)
        share = 1.0 / (1.0 + jnp.exp(-gap))
        mixed = (share * near[:, :width] + (1.0 - share) * far[:, :width]).astype(BF16)
        resid = halves(x_ref[...].astype(F32)) + dot(mixed, wo_ref[...])
        acc[...] = resid
        n2s[...] = norm_rows(resid, gain_ref[...]).astype(BF16)
        fetch[0].wait()

    @pl.when(step > 0)
    def _():
        at = pl.multiple_of((step - 1) * 256, 256)

        def place(index):
            return here * rows + at + (index % 8) * 32 + index // 8

        n2 = n2s[pl.ds(at, 256), :]
        total = acc[pl.ds(at, 256), :]
        chunk = 512
        hidden = w1.shape[1]
        us[0] = dot(n2, w1[:, :chunk])

        @pl.when(step == 1)
        def _():
            for copy in fetch[1:]:
                copy.wait()

        ahead = us[0]
        for f in range(hidden // chunk):
            u = ahead
            if (f + 1) * chunk < hidden:
                ahead = dot(n2, w1[:, (f + 1) * chunk : (f + 2) * chunk])
            total = total + dot(gelu(u).astype(BF16), w2[f * chunk : (f + 1) * chunk, :])
        live = place(lax.broadcasted_iota(jnp.int32, (256, 1), 0)) < count
        enc32 = jnp.where(live, total, 0.0).astype(BF16).astype(F32)
        enc = enc32.astype(BF16)
        enc_ref[...] = enc32.reshape(enc_ref.shape).astype(BF16)
        encs[pl.ds(at, 256), :] = enc
        z = dot(enc, pool[...].reshape(width, width))
        hidden = width // 2
        gate = jnp.tanh(z[:, :hidden]) * (1.0 / (1.0 + jnp.exp(-z[:, hidden:])))
        g_hi, g_mid, g_lo = thirds(gate)
        stack = jnp.concatenate(thirds(cw_ref[...]), 0).astype(BF16)
        one = dot_nt(stack, g_hi.astype(BF16))
        two = dot_nt(stack[:16], g_mid.astype(BF16))
        three = dot_nt(stack[:16], g_lo.astype(BF16))
        logits = one[0:8] + ((one[8:16] + two[0:8]) + (one[16:24] + two[8:16] + three[0:8]))
        live_t = place(lax.broadcasted_iota(jnp.int32, (1, 256), 1)) < count
        logit[:, pl.ds(at, 256)] = jnp.where(live_t, logits, -1e30)

    @pl.when(step == 2)
    def _():
        every = logit[...]
        peak = jnp.max(every, axis=1, keepdims=True)
        e = jnp.where(every > -1e29, jnp.exp(every - peak), 0.0)
        total = jnp.sum(e, axis=1, keepdims=True)
        numer = dot(jnp.concatenate(thirds(e), 0).astype(BF16), encs[...])
        numer = numer[0:8] + (numer[8:16] + numer[16:24])
        mine = packed(peak, total, numer)
        if slide:
            other = other_ref[...]
            red_ref[0] = jnp.where(core_ref[0] == 0, other, mine)
            red_ref[1] = jnp.where(core_ref[0] == 0, mine, other)
        else:
            red_ref[...] = mine


def finish(slide, where, x, near, back, wo, gain, w1, w2, wp, cw, other=None):
    classes, _, tall, width = x.shape
    rows = classes * tall
    hidden = w1.shape[1]
    once = pl.Buffered(1)
    if slide:
        red = jax.ShapeDtypeStruct((2, 8, WIDE), F32)
    else:
        red = pltpu.HBM((8, WIDE), F32)
    extra = [pl.BlockSpec((8, WIDE), lambda i, *_: (0, 0))] if slide else []
    return pl.pallas_call(
        functools.partial(post, slide),
        out_shape=(pltpu.HBM((classes, tall, width), BF16), red),
        grid_spec=pltpu.PrefetchScalarGridSpec(
            num_scalar_prefetch=4,
            grid=(3,),
            in_specs=[
                pl.BlockSpec(
                    (classes, None, tall, width), lambda i, *_: (0, slide, 0, 0), pipeline_mode=once
                ),
                pl.BlockSpec((rows, WIDE), lambda i, *_: (0, 0), pipeline_mode=once),
                pl.BlockSpec((classes, tall, WIDE), lambda i, *_: (0, 0, 0), pipeline_mode=once),
                pl.BlockSpec((width, width), lambda i, *_: (0, 0), pipeline_mode=once),
                pl.BlockSpec((1, width), lambda i, *_: (0, 0)),
                *[pl.BlockSpec(memory_space=pltpu.HBM)] * 6,
                pl.BlockSpec((8, width // 2), lambda i, *_: (0, 0)),
                *extra,
            ],
            out_specs=(
                pl.BlockSpec((classes, 8, width), lambda i, *_: (0, jnp.maximum(i - 1, 0), 0)),
                pl.BlockSpec(red.shape, lambda i, *_: (0,) * len(red.shape)),
            ),
            scratch_shapes=[
                pltpu.VMEM((rows, width), BF16),
                pltpu.VMEM((rows, width), F32),
                pltpu.VMEM((rows, width), BF16),
                pltpu.VMEM((1, 256, 512), F32),
                pltpu.VMEM((8, rows), F32),
                pltpu.VMEM((width, hidden), BF16),
                pltpu.VMEM((hidden, width), BF16),
                pltpu.VMEM((4, width // 4, width), BF16),
                pltpu.SemaphoreType.DMA((6,)),
            ],
        ),
        compiler_params=pltpu.CompilerParams(vmem_limit_bytes=34 << 20),
        cost_estimate=pl.CostEstimate(
            flops=2 * rows * width * (2 * width + 2 * hidden),
            bytes_accessed=4 * width * (width + hidden) + 8 * rows * width,
            transcendentals=rows * hidden,
        ),
        name="post",
    )(*where, x, near, back, wo, gain, w1, w2, *wp, cw, *([other] if slide else []))


def merged(x):
    width = x.shape[2] - 128
    tail = x[:, :, width:].astype(F32)
    at = lax.broadcasted_iota(jnp.int32, tail.shape, 2)
    peak = jnp.sum(jnp.where(at < 3, tail, 0.0), axis=2, keepdims=True)
    total = jnp.sum(jnp.where((at >= 3) & (at < 6), tail, 0.0), axis=2, keepdims=True)
    top = jnp.max(peak, axis=0, keepdims=True)
    w = jnp.exp(peak - top)
    numer = jnp.sum(w * x[:, :, :width].astype(F32), axis=0)
    return top[0], jnp.sum(w * total, axis=0), numer


def packed(peak, total, numer):
    tail = jnp.zeros((8, 128), F32)
    at = lax.broadcasted_iota(jnp.int32, (8, 128), 1)
    for k, piece in enumerate((*thirds(peak), *thirds(total))):
        tail = jnp.where(at == k, piece, tail)
    return jnp.concatenate([numer, tail], 1)


def fold_some(last, *refs):
    *pieces, out_ref = refs
    peak, total, numer = merged(jnp.concatenate([p[...] for p in pieces], 0))
    if last:
        out_ref[0] = numer / total
    else:
        out_ref[0] = packed(peak, total, numer)


def joined(pair, core):
    swap = [(0, 1), (1, 0)]

    def fold(pieces, last):
        wide = WIDE - 128 if last else WIDE
        return pl.pallas_call(
            functools.partial(fold_some, last),
            out_shape=jax.ShapeDtypeStruct((1, 8, wide), F32),
            grid=(1,),
            in_specs=[pl.BlockSpec((1, 8, WIDE), lambda i: (0, 0, 0))] * len(pieces),
            out_specs=pl.BlockSpec((1, 8, wide), lambda i: (0, 0, 0)),
            compiler_params=pltpu.CompilerParams(vmem_limit_bytes=8 << 20),
            name="fold",
        )(*pieces)

    piece = fold([pair, lax.ppermute(pair[1:], SEQ[2], swap)], False)
    for axis in SEQ[1::-1]:
        size = lax.axis_size(axis)
        sent = [
            lax.ppermute(piece, axis, [(i, (i + k) % size) for i in range(size)])
            for k in range(1, size)
        ]
        piece = fold([piece, *sent], axis == SEQ[0])
    theirs = lax.ppermute(piece, SEQ[2], swap)
    first = core == 0
    both = [jnp.where(first, piece, theirs), jnp.where(first, theirs, piece)]
    return jnp.concatenate(both, 0)


def exchange(x):
    return lax.all_to_all(x, SEQ, 0, 0, tiled=True)


def layer(
    tiles,
    counts,
    ln1_gain,
    qkv_weight,
    out_weight,
    ln2_gain,
    ff_in,
    ff_out,
    pool_weight,
    class_weight,
):
    slides, rows, width = tiles.shape
    ratio = lax.axis_size(SEQ)
    here = lax.axis_index(SEQ)
    where = (here.astype(jnp.int32).reshape(1), counts)
    gain1, gain2 = ln1_gain.reshape(1, width), ln2_gain.reshape(1, width)
    mine = jnp.transpose(
        tiles.reshape(slides, rows // ratio, ratio, width), (2, 0, 1, 3)
    )
    moved = exchange(mine)
    mine_at = lax.axis_index("grp")
    core = lax.axis_index(SEQ[2])
    quarters = [pool_weight]
    for k in (1, 2, 3):
        quarters.append(lax.ppermute(pool_weight, "grp", [(i, (i + k) % 4) for i in range(4)]))
    whole = [pltpu.with_memory_space_constraint(q, pltpu.HBM) for q in quarters]
    qkv_weight, out_weight, ff_in, ff_out = (
        pltpu.with_memory_space_constraint(w, pltpu.HBM)
        for w in (qkv_weight, out_weight, ff_in, ff_out)
    )
    near = []
    for s in range(slides):
        out = attend(True, s, where, mine, gain1, qkv_weight)
        near.append(pltpu.with_memory_space_constraint(out, pltpu.HBM))
    back = []
    for s in range(slides):
        far = attend(False, s, where, moved, gain1, qkv_weight)
        back.append(exchange(far.reshape(ratio, rows // ratio, WIDE)))
    encoded, partial = [], []
    for s in range(slides):
        enc, red = finish(
            s, (*where, mine_at.astype(jnp.int32).reshape(1), core.astype(jnp.int32).reshape(1)), mine, near[s], back[s], out_weight, gain2, ff_in, ff_out, whole,
            class_weight.T, *partial,
        )
        encoded.append(jnp.swapaxes(enc, 0, 1).reshape(rows, width))
        partial.append(red if s else pltpu.with_memory_space_constraint(red, pltpu.HBM))
    pooled = joined(partial[1], core)
    return (jnp.stack(encoded), pooled)


def solution(mesh):
    torus = Mesh(
        mesh.devices.reshape(mesh.shape["grp"], 4, 4, 2), ("grp", "seq_0", "seq_1", "seq_2")
    )
    return jax.shard_map(
        layer,
        mesh=torus,
        in_specs=(P("grp", SEQ, None), P("grp"), P(), P(), P(), P(), P(), P(), P("grp", None), P()),
        out_specs=(P("grp", SEQ, None), P("grp", None, None)),
        check_vma=False,
    )
```

```python
import functools

import jax
import jax.numpy as jnp
from jax import lax
from jax.experimental import pallas as pl
from jax.experimental.pallas import tpu as pltpu
from jax.sharding import Mesh
from jax.sharding import PartitionSpec as P


HEADS = 16
BLOCK = 256
WIDE = 896
SEQ = ("seq_0", "seq_1", "seq_2")
F32 = jnp.float32
BF16 = jnp.bfloat16
LOG2E = 1.4426950408889634
LN2 = 0.6931471805599453


def dot(a, b):
    return jnp.dot(a, b, preferred_element_type=F32)


def dot_nt(a, b):
    return lax.dot_general(a, b, (((1,), (1,)), ((), ())), preferred_element_type=F32)


def norm_rows(x, gain):
    centre = jnp.mean(x, axis=-1, keepdims=True)
    c = x - centre
    spread = jnp.mean(c * c, axis=-1, keepdims=True)
    return c * lax.rsqrt(spread + 1e-05) * gain


def thirds(x):
    hi = x.astype(BF16).astype(F32)
    rest = x - hi
    mid = rest.astype(BF16).astype(F32)
    return hi, mid, (rest - mid).astype(BF16).astype(F32)


def attention(near, slide, here_ref, counts_ref, x_ref, gain_ref, w_ref, out_ref, nrm, qs, ks, vt, ot, lt, sc, mx, ps):
    step = pl.program_id(0)
    here, count = here_ref[0], counts_ref[slide]
    rows, width = nrm.shape
    head_dim = width // HEADS
    half = HEADS // 2
    span = half * head_dim

    def place(index):
        if near:
            block, rest = index // 256, index % 256
            return here * rows + block * 256 + (rest % 8) * 32 + rest // 8
        return index * 32 + here

    @pl.when(step == 0)
    def _():
        x = x_ref[...].astype(F32)
        pos = place(lax.broadcasted_iota(jnp.int32, (rows, 1), 0))
        if near:
            x = jnp.concatenate(
                [x[:, 8 * b : 8 * b + 8].reshape(rows // 2, width) for b in range(2)], 0
            )
            first = jnp.concatenate(
                [jnp.broadcast_to(x[b * 256 : b * 256 + 1], (256, width)) for b in range(2)], 0
            )
        else:
            x = x.reshape(rows, width)
            first = jnp.broadcast_to(x[0:1], x.shape)
        x = jnp.where(pos < count, x, first)
        for part in (slice(0, rows // 2), slice(rows // 2, rows)):
            nrm[part] = norm_rows(x[part], gain_ref[...]).astype(BF16)
            qs[part] = dot(nrm[part], w_ref[...]).astype(BF16)

    @pl.when(step == 1)
    def _():
        ks[...] = dot(nrm[...], w_ref[...]).astype(BF16)

    @pl.when(step == 2)
    def _():
        v = dot(nrm[...], w_ref[...])
        live = place(lax.broadcasted_iota(jnp.int32, (1, rows), 1)) < count
        values = jnp.where(live, v.T, 0.0).astype(BF16)
        ones = jnp.where(
            lax.broadcasted_iota(jnp.int32, (16, rows), 0) == 0, jnp.where(live, 1.0, 0.0), 0.0
        ).astype(BF16)
        for h in range(HEADS):
            vt[h // half, h % half, :head_dim] = values[h * head_dim : (h + 1) * head_dim]
            vt[h // half, h % half, head_dim:] = ones
        scale = LOG2E / head_dim**0.5
        keys = BLOCK if near else rows

        def corner(i):
            g, t = i // 2, i % 2
            qrow = pl.multiple_of(t * 256, 256)
            return g, pl.multiple_of(g * span, 128), qrow, qrow if near else 0

        def scores(i, hh):
            _, base, qrow, krow = corner(i)
            off = hh * head_dim
            w0 = off // 128 * 128
            wide = 128 if off + head_dim <= w0 + 128 else 256
            lane = lax.broadcasted_iota(jnp.int32, (1, wide), 1) + w0
            inside = jnp.where((lane >= off) & (lane < off + head_dim), 1.0, 0.0).astype(BF16)
            cols = pl.ds(base + w0, wide)
            kh = ks[pl.ds(krow, keys), cols] * inside
            s = dot_nt(kh, qs[pl.ds(qrow, 256), cols])
            sc[hh % 2] = s
            mx[hh % 4] = jnp.max(s, axis=0, keepdims=True) * scale

        def weights(hh):
            s = sc[hh % 2]
            ps[hh % 2] = jnp.exp2(s * scale - mx[hh % 4]).astype(BF16)

        def mix(i, hh):
            g, _, qrow, krow = corner(i)
            off = hh * head_dim
            o = dot(vt[g, hh, :, pl.ds(krow, keys)], ps[hh % 2])
            total = jnp.maximum(o[head_dim : head_dim + 1], 1e-30)
            ot[g, off : off + head_dim, pl.ds(qrow, 256)] = o[:head_dim] * (1.0 / total)
            lt[g, hh : hh + 1, pl.ds(qrow, 256)] = (mx[hh % 4] + jnp.log2(total)) * LN2

        def part(i, carry):
            for hh in range(half):
                if hh + 1 < half:
                    scores(i, hh + 1)
                else:
                    scores(lax.rem(i + 1, 4), 0)
                if hh:
                    mix(i, hh - 1)
                else:
                    mix(lax.rem(i + 3, 4), half - 1)
                weights(hh)
            return carry

        scores(0, 0)
        lax.fori_loop(0, 4, part, 0)
        mix(3, half - 1)
        out_ref[:, :width] = ot[...].reshape(width, rows).T.astype(out_ref.dtype)
        pieces = thirds(lt[...].reshape(HEADS, rows))
        tail = jnp.concatenate([*pieces, jnp.zeros((128 - 3 * HEADS, rows), F32)], 0)
        out_ref[:, width:] = tail.T.astype(out_ref.dtype)


def attend(near, slide, where, x, gain, weight):
    classes, _, tall, width = x.shape
    rows = classes * tall
    keys = BLOCK if near else rows
    return pl.pallas_call(
        functools.partial(attention, near, slide),
        out_shape=pltpu.HBM((rows, WIDE), F32 if near else BF16),
        grid_spec=pltpu.PrefetchScalarGridSpec(
            num_scalar_prefetch=2,
            grid=(3,),
            in_specs=[
                pl.BlockSpec((classes, None, tall, width), lambda i, *_: (0, slide, 0, 0)),
                pl.BlockSpec((1, width), lambda i, *_: (0, 0)),
                pl.BlockSpec((width, width), lambda i, *_: (0, i)),
            ],
            out_specs=pl.BlockSpec((rows, WIDE), lambda i, *_: (0, 0)),
            scratch_shapes=[
                pltpu.VMEM((rows, width), BF16),
                pltpu.VMEM((rows, width), BF16),
                pltpu.VMEM((rows, width), BF16),
                pltpu.VMEM((2, HEADS // 2, width // HEADS + 16, rows), BF16),
                pltpu.VMEM((2, width // 2, rows), F32),
                pltpu.VMEM((2, HEADS // 2, rows), F32),
                pltpu.VMEM((2, keys, 256), F32),
                pltpu.VMEM((4, 1, 256), F32),
                pltpu.VMEM((2, keys, 256), BF16),
            ],
        ),
        compiler_params=pltpu.CompilerParams(vmem_limit_bytes=20 << 20),
        cost_estimate=pl.CostEstimate(
            flops=2 * rows * width * (3 * width + 2 * keys),
            bytes_accessed=2 * 3 * width * width + 6 * rows * width,
            transcendentals=rows * keys * HEADS,
        ),
        name="near" if near else "far",
    )(*where, x, gain, weight)


def gelu(x):
    return 0.5 * x * (1.0 + lax.erf(x * 0.7071067811865476))


def post(slide, here_ref, counts_ref, grp_ref, core_ref, *refs):
    x_ref, near_ref, far_ref, wo_ref, gain_ref, w1_ref, w2_ref, *refs = refs
    *wp_refs, cw_ref = refs[:5]
    refs = refs[5:]
    if slide:
        other_ref, *refs = refs
    enc_ref, red_ref, n2s, acc, encs, us, logit, w1, w2, pool, sem = refs
    step = pl.program_id(0)
    here, count = here_ref[0], counts_ref[slide]
    width = wo_ref.shape[0]
    head_dim = width // HEADS
    rows = acc.shape[0]
    fetch = [pltpu.make_async_copy(w1_ref, w1, sem.at[4]), pltpu.make_async_copy(w2_ref, w2, sem.at[5])] + [
        pltpu.make_async_copy(wp_refs[k], pool.at[lax.rem(grp_ref[0] - k + 4, 4)], sem.at[k])
        for k in range(4)
    ]

    @pl.when(step == 0)
    def _():
        for copy in fetch:
            copy.start()

    @pl.when(step < 2)
    def _():
        head = lax.broadcasted_iota(jnp.int32, (HEADS, width), 0) * head_dim
        lane = lax.broadcasted_iota(jnp.int32, (HEADS, width), 1)
        hit = jnp.where((lane >= head) & (lane < head + head_dim), 1.0, 0.0)
        rest = jnp.zeros((128 - 3 * HEADS, width), F32)
        spread = jnp.concatenate([hit, hit, hit, rest, -hit, -hit, -hit, rest], 0).astype(BF16)
        at = pl.ds(pl.multiple_of(step * 256, 256), 256)
        far = far_ref[...].astype(F32).reshape(256, WIDE)
        near = near_ref[...]
        parts = jnp.concatenate([near[:, width:], far[:, width:]], 1).astype(BF16)
        gap = dot(parts, spread)
        share = 1.0 / (1.0 + jnp.exp(-gap))
        mixed = (share * near[:, :width] + (1.0 - share) * far[:, :width]).astype(BF16)
        resid = x_ref[...].astype(F32).reshape(256, width) + dot(mixed, wo_ref[...])
        acc[at, :] = resid
        n2s[at, :] = norm_rows(resid, gain_ref[...]).astype(BF16)

    @pl.when(step == 1)
    def _():
        fetch[0].wait()

    @pl.when(step > 1)
    def _():
        at = pl.multiple_of((step - 2) * 256, 256)

        def place(index):
            return here * rows + at + (index % 8) * 32 + index // 8

        n2 = n2s[pl.ds(at, 256), :]
        total = acc[pl.ds(at, 256), :]
        chunk = 512
        hidden = w1.shape[1]
        us[0] = dot(n2, w1[:, :chunk])

        @pl.when(step == 2)
        def _():
            for copy in fetch[1:]:
                copy.wait()

        ahead = us[0]
        for f in range(hidden // chunk):
            u = ahead
            if (f + 1) * chunk < hidden:
                ahead = dot(n2, w1[:, (f + 1) * chunk : (f + 2) * chunk])
            total = total + dot(gelu(u).astype(BF16), w2[f * chunk : (f + 1) * chunk, :])
        live = place(lax.broadcasted_iota(jnp.int32, (256, 1), 0)) < count
        enc32 = jnp.where(live, total, 0.0).astype(BF16).astype(F32)
        enc = enc32.astype(BF16)
        enc_ref[...] = enc32.reshape(enc_ref.shape).astype(BF16)
        encs[pl.ds(at, 256), :] = enc
        z = dot(enc, pool[...].reshape(width, width))
        hidden = width // 2
        gate = jnp.tanh(z[:, :hidden]) * (1.0 / (1.0 + jnp.exp(-z[:, hidden:])))
        g_hi, g_mid, g_lo = thirds(gate)
        stack = jnp.concatenate(thirds(cw_ref[...]), 0).astype(BF16)
        one = dot_nt(stack, g_hi.astype(BF16))
        two = dot_nt(stack[:16], g_mid.astype(BF16))
        three = dot_nt(stack[:16], g_lo.astype(BF16))
        logits = one[0:8] + ((one[8:16] + two[0:8]) + (one[16:24] + two[8:16] + three[0:8]))
        live_t = place(lax.broadcasted_iota(jnp.int32, (1, 256), 1)) < count
        logit[:, pl.ds(at, 256)] = jnp.where(live_t, logits, -1e30)

    @pl.when(step == 3)
    def _():
        every = logit[...]
        peak = jnp.max(every, axis=1, keepdims=True)
        e = jnp.where(every > -1e29, jnp.exp(every - peak), 0.0)
        total = jnp.sum(e, axis=1, keepdims=True)
        numer = dot(jnp.concatenate(thirds(e), 0).astype(BF16), encs[...])
        numer = numer[0:8] + (numer[8:16] + numer[16:24])
        mine = packed(peak, total, numer)
        if slide:
            other = other_ref[...]
            red_ref[0] = jnp.where(core_ref[0] == 0, other, mine)
            red_ref[1] = jnp.where(core_ref[0] == 0, mine, other)
        else:
            red_ref[...] = mine


def finish(slide, where, x, near, back, wo, gain, w1, w2, wp, cw, other=None):
    classes, _, tall, width = x.shape
    rows = classes * tall
    hidden = w1.shape[1]
    once = pl.Buffered(1)
    if slide:
        red = jax.ShapeDtypeStruct((2, 8, WIDE), F32)
    else:
        red = pltpu.HBM((8, WIDE), F32)
    extra = [pl.BlockSpec((8, WIDE), lambda i, *_: (0, 0))] if slide else []
    return pl.pallas_call(
        functools.partial(post, slide),
        out_shape=(pltpu.HBM((classes, tall, width), BF16), red),
        grid_spec=pltpu.PrefetchScalarGridSpec(
            num_scalar_prefetch=4,
            grid=(4,),
            in_specs=[
                pl.BlockSpec(
                    (classes, None, 8, width), lambda i, *_: (0, slide, jnp.minimum(i, 1), 0)
                ),
                pl.BlockSpec((rows // 2, WIDE), lambda i, *_: (jnp.minimum(i, 1), 0)),
                pl.BlockSpec((classes, 8, WIDE), lambda i, *_: (0, jnp.minimum(i, 1), 0)),
                pl.BlockSpec((width, width), lambda i, *_: (0, 0), pipeline_mode=once),
                pl.BlockSpec((1, width), lambda i, *_: (0, 0)),
                *[pl.BlockSpec(memory_space=pltpu.HBM)] * 6,
                pl.BlockSpec((8, width // 2), lambda i, *_: (0, 0)),
                *extra,
            ],
            out_specs=(
                pl.BlockSpec((classes, 8, width), lambda i, *_: (0, jnp.maximum(i - 2, 0), 0)),
                pl.BlockSpec(red.shape, lambda i, *_: (0,) * len(red.shape)),
            ),
            scratch_shapes=[
                pltpu.VMEM((rows, width), BF16),
                pltpu.VMEM((rows, width), F32),
                pltpu.VMEM((rows, width), BF16),
                pltpu.VMEM((1, 256, 512), F32),
                pltpu.VMEM((8, rows), F32),
                pltpu.VMEM((width, hidden), BF16),
                pltpu.VMEM((hidden, width), BF16),
                pltpu.VMEM((4, width // 4, width), BF16),
                pltpu.SemaphoreType.DMA((6,)),
            ],
        ),
        compiler_params=pltpu.CompilerParams(vmem_limit_bytes=34 << 20),
        cost_estimate=pl.CostEstimate(
            flops=2 * rows * width * (2 * width + 2 * hidden),
            bytes_accessed=4 * width * (width + hidden) + 8 * rows * width,
            transcendentals=rows * hidden,
        ),
        name="post",
    )(*where, x, near, back, wo, gain, w1, w2, *wp, cw, *([other] if slide else []))


def merged(x):
    width = x.shape[2] - 128
    tail = x[:, :, width:].astype(F32)
    at = lax.broadcasted_iota(jnp.int32, tail.shape, 2)
    peak = jnp.sum(jnp.where(at < 3, tail, 0.0), axis=2, keepdims=True)
    total = jnp.sum(jnp.where((at >= 3) & (at < 6), tail, 0.0), axis=2, keepdims=True)
    top = jnp.max(peak, axis=0, keepdims=True)
    w = jnp.exp(peak - top)
    numer = jnp.sum(w * x[:, :, :width].astype(F32), axis=0)
    return top[0], jnp.sum(w * total, axis=0), numer


def packed(peak, total, numer):
    tail = jnp.zeros((8, 128), F32)
    at = lax.broadcasted_iota(jnp.int32, (8, 128), 1)
    for k, piece in enumerate((*thirds(peak), *thirds(total))):
        tail = jnp.where(at == k, piece, tail)
    return jnp.concatenate([numer, tail], 1)


def fold_some(last, *refs):
    *pieces, out_ref = refs
    peak, total, numer = merged(jnp.concatenate([p[...] for p in pieces], 0))
    if last:
        out_ref[0] = numer / total
    else:
        out_ref[0] = packed(peak, total, numer)


def joined(pair, core):
    swap = [(0, 1), (1, 0)]

    def fold(pieces, last):
        wide = WIDE - 128 if last else WIDE
        return pl.pallas_call(
            functools.partial(fold_some, last),
            out_shape=jax.ShapeDtypeStruct((1, 8, wide), F32),
            grid=(1,),
            in_specs=[pl.BlockSpec((1, 8, WIDE), lambda i: (0, 0, 0))] * len(pieces),
            out_specs=pl.BlockSpec((1, 8, wide), lambda i: (0, 0, 0)),
            compiler_params=pltpu.CompilerParams(vmem_limit_bytes=8 << 20),
            name="fold",
        )(*pieces)

    piece = fold([pair, lax.ppermute(pair[1:], SEQ[2], swap)], False)
    for axis in SEQ[1::-1]:
        size = lax.axis_size(axis)
        sent = [
            lax.ppermute(piece, axis, [(i, (i + k) % size) for i in range(size)])
            for k in range(1, size)
        ]
        piece = fold([piece, *sent], axis == SEQ[0])
    theirs = lax.ppermute(piece, SEQ[2], swap)
    first = core == 0
    both = [jnp.where(first, piece, theirs), jnp.where(first, theirs, piece)]
    return jnp.concatenate(both, 0)


def exchange(x):
    return lax.all_to_all(x, SEQ, 0, 0, tiled=True)


def layer(
    tiles,
    counts,
    ln1_gain,
    qkv_weight,
    out_weight,
    ln2_gain,
    ff_in,
    ff_out,
    pool_weight,
    class_weight,
):
    slides, rows, width = tiles.shape
    ratio = lax.axis_size(SEQ)
    here = lax.axis_index(SEQ)
    where = (here.astype(jnp.int32).reshape(1), counts)
    gain1, gain2 = ln1_gain.reshape(1, width), ln2_gain.reshape(1, width)
    mine = jnp.transpose(
        tiles.reshape(slides, rows // ratio, ratio, width), (2, 0, 1, 3)
    )
    moved = exchange(mine)
    mine_at = lax.axis_index("grp")
    core = lax.axis_index(SEQ[2])
    quarters = [pool_weight]
    for k in (1, 2, 3):
        quarters.append(lax.ppermute(pool_weight, "grp", [(i, (i + k) % 4) for i in range(4)]))
    whole = [pltpu.with_memory_space_constraint(q, pltpu.HBM) for q in quarters]
    qkv_weight, out_weight, ff_in, ff_out = (
        pltpu.with_memory_space_constraint(w, pltpu.HBM)
        for w in (qkv_weight, out_weight, ff_in, ff_out)
    )
    near = []
    for s in range(slides):
        out = attend(True, s, where, mine, gain1, qkv_weight)
        near.append(pltpu.with_memory_space_constraint(out, pltpu.HBM))
    back = []
    for s in range(slides):
        far = attend(False, s, where, moved, gain1, qkv_weight)
        back.append(exchange(far.reshape(ratio, rows // ratio, WIDE)))
    encoded, partial = [], []
    for s in range(slides):
        enc, red = finish(
            s, (*where, mine_at.astype(jnp.int32).reshape(1), core.astype(jnp.int32).reshape(1)), mine, near[s], back[s], out_weight, gain2, ff_in, ff_out, whole,
            class_weight.T, *partial,
        )
        encoded.append(jnp.swapaxes(enc, 0, 1).reshape(rows, width))
        partial.append(red if s else pltpu.with_memory_space_constraint(red, pltpu.HBM))
    pooled = joined(partial[1], core)
    return (jnp.stack(encoded), pooled)


def solution(mesh):
    torus = Mesh(
        mesh.devices.reshape(mesh.shape["grp"], 4, 4, 2), ("grp", "seq_0", "seq_1", "seq_2")
    )
    return jax.shard_map(
        layer,
        mesh=torus,
        in_specs=(P("grp", SEQ, None), P("grp"), P(), P(), P(), P(), P(), P(), P("grp", None), P()),
        out_specs=(P("grp", SEQ, None), P("grp", None, None)),
        check_vma=False,
    )
```
